32 devices in a mesh: dp: 8 (over z, x), row: 2 (over y), col: 2 (over core).
Axes of the slice: x: 2, y: 2, z: 4, core: 2. Of those that a mesh axis runs over, the one named last changes fastest.
Arguments:
- block_input: bfloat16 [4096, 768], P(('dp', 'row'), 'col'), may hold values from -27 to 27
- cotangent: bfloat16 [4096, 768], P(('dp', 'row'), 'col'), may hold values from -6 to 6
- segment_ids: int32 [16, 256], P(('dp', 'col')), may hold values from 0 to 2, never falling along the last dimension, each value on 1 to 153 neighbouring positions
- first_gain: float32 [768], P('col'), may hold values from 0.5 to 1.5
- first_shift: float32 [768], P('col'), may hold values from -3 to 3
- input_weight: bfloat16 [768, 3, 768], P('col', None, 'row'), may hold values from -0.21875 to 0.21875
- query_value_bias: float32 [2, 768], P(None, 'row'), may hold values from -3 to 3
- output_weight: bfloat16 [768, 768], P('row', 'col'), may hold values from -1.5 to 1.5
- output_bias: float32 [768], P('col'), may hold values from -3 to 3
- second_gain: float32 [768], P('col'), may hold values from 0.5 to 1.5
- second_shift: float32 [768], P('col'), may hold values from -3 to 3
- hidden_weight: bfloat16 [768, 3072], P('col', 'row'), may hold values from -0.25 to 0.25
- hidden_bias: float32 [3072], P('row'), may hold values from -3 to 3
- return_weight: bfloat16 [3072, 768], P('row', 'col'), may hold values from -0.21875 to 0.21875
- return_bias: float32 [768], P('col'), may hold values from -3 to 3
Outputs:
- block_output: bfloat16 [4096, 768], P(('dp', 'row'), 'col')
- input_grad: bfloat16 [4096, 768], P(('dp', 'row'), 'col')
- first_gain_grad: float32 [768], P('col')
- first_shift_grad: float32 [768], P('col')
- input_weight_grad: float32 [768, 3, 768], P('col', None, 'row')
- query_value_bias_grad: float32 [2, 768], P(None, 'row')
- output_weight_grad: float32 [768, 768], P('row', 'col')
- output_bias_grad: float32 [768], P('col')
- second_gain_grad: float32 [768], P('col')
- second_shift_grad: float32 [768], P('col')
- hidden_weight_grad: float32 [768, 3072], P('col', 'row')
- hidden_bias_grad: float32 [3072], P('row')
- return_weight_grad: float32 [3072, 768], P('row', 'col')
- return_bias_grad: float32 [768], P('col')
The draws below stay inside these ranges and needn't reach their ends.
Inputs may be any that keep to these rules, and one draw needn't show every extreme that they name: `segment_ids`: within each sequence the numbers never fall; each document holds 1 to 153 tokens.
All inputs are finite; a program needn't handle non-finite values.
Results may differ from the reference program's by a relative error of at most 0.03.
Values may be sent and summed in bfloat16 or wider, within the bound.
No kernel may reach another device: no remote copies, remote signals or barrier semaphores. Data moves between devices by JAX's collectives and lax.ppermute only.
A program may use at most 64 MiB of HBM per device.

```python
import math
import jax
import jax.numpy as jnp
import numpy as np
from jax import lax

D = 768
HEADS = 12
HEAD = 64
FF = 3072
SEQ = 256
SEQS = 16
TOKENS = 4096


def draw_block_input(key, part):
    noise_key, row_key, col_key = jax.random.split(key, 3)
    row_scale = jnp.exp(jax.random.uniform(row_key, (TOKENS, 1), jnp.float32, math.log(0.3), math.log(3.0)))
    col_scale = jnp.exp(jax.random.uniform(col_key, (1, D), jnp.float32, math.log(0.3), math.log(3.0)))
    noise_vals = jax.random.truncated_normal(noise_key, -3.0, 3.0, (TOKENS, D), jnp.float32)
    return (noise_vals * row_scale * col_scale).astype(jnp.bfloat16)


def draw_hidden_weight(key, part):
    noise_key, sign_key = jax.random.split(jax.random.fold_in(key, 17))
    feature = jnp.arange(D).astype(jnp.float32)
    ramp = (2.0 * (feature + 0.5) / D - 1.0) * 1.7
    sign_val = jnp.where(jax.random.bernoulli(sign_key, 0.5), 1.0, -1.0).astype(jnp.float32)
    offset = sign_val * (1.5 / math.sqrt(D)) * ramp
    noise_vals = jax.random.truncated_normal(noise_key, -4.5, 4.5, (D, FF), jnp.float32)
    values = noise_vals / math.sqrt(D) + offset[:, None]
    return jnp.clip(values, -0.25, 0.25).astype(jnp.bfloat16)


def levels(rng, shape, shards, smallest, high):
    level = 1.0
    for position, parts in shards:
        draws = jax.random.uniform(jax.random.fold_in(jax.random.fold_in(rng, 6), position), (parts,), jnp.float32, smallest / len(shards), high / len(shards))
        level = level * jnp.repeat(jnp.exp(draws), shape[position] // parts).reshape((-1,) + (1,) * (len(shape) - 1 - position))
    return level


def length_profile(count, total, limit, lean):
    weights = [(1 << 20) // math.isqrt(standing ** lean) + 1 for standing in range(2, count + 1)]
    rest, holding = total - limit - (count - 1), [1] * (count - 1)
    while rest > 0:
        movable = [i for i in range(count - 1) if holding[i] < limit]
        mass, budget = sum([weights[i] for i in movable]), rest
        for i in movable:
            more = min(limit - holding[i], max(1, budget * weights[i] // mass), rest)
            holding[i] = holding[i] + more
            rest = rest - more
    return np.array([limit] + holding)


def uneven_parts(rng, count, total, bound, skew):
    if count == 2:
        one = jax.random.randint(rng, (), max(1, total - bound), min(bound, total - 1) + 1)
        return jnp.stack([one, total - one])
    sizes = jnp.asarray(length_profile(count, total, bound, skew), jnp.int32)
    pairs = (count - 1) // 2
    donor, taker = sizes[1:1 + 2 * pairs:2], sizes[2:2 + 2 * pairs:2]
    margin = jnp.minimum(donor - 1, bound - taker)
    passed = jax.random.randint(jax.random.fold_in(rng, 1), (pairs,), 0, 1 << 20) % (margin + 1)
    sizes = sizes.at[1:1 + 2 * pairs:2].set(donor - passed).at[2:2 + 2 * pairs:2].set(taker + passed)
    return sizes[jax.random.permutation(jax.random.fold_in(rng, 2), count)]


def scatter_about(rng, dims, scale, most, shards=(), held_as=jnp.bfloat16):
    drawn = scale * jax.random.normal(rng, dims, jnp.float32)
    if shards:
        drawn = drawn * levels(rng, dims, shards, -0.22, 0.18)
    return jnp.clip(drawn, -most, most).astype(held_as)


def setup_inputs(seed: int = 0) -> dict:
    key_of = jax.random.split(jax.random.key(seed), 16)
    return {
        "block_input": draw_block_input(jax.random.fold_in(key_of[15], 71), 0),
        "cotangent": scatter_about(key_of[1], (TOKENS, D), 1.0, 6.0, ((0, 16), (1, 2))),
        "segment_ids": jax.vmap(lambda own: jnp.searchsorted(jnp.cumsum(uneven_parts(own, 3, SEQ, SEQ // 2 + SEQ // 10, 0)), jnp.arange(SEQ), side="right"))(jax.random.split(key_of[2], SEQS)).reshape((SEQS, SEQ)).astype(jnp.int32),
        "first_gain": jnp.clip(1.0 + 0.1 * jax.random.normal(key_of[3], (D,), jnp.float32), 0.5, 1.5),
        "first_shift": scatter_about(key_of[4], (D,), 0.5, 3.0, ((0, 2),), jnp.float32),
        "input_weight": scatter_about(key_of[5], (D, 3, D), D ** -0.5, 0.21875, ((0, 2), (2, 2))),
        "query_value_bias": scatter_about(key_of[6], (2, D), 0.5, 3.0, ((1, 2),), jnp.float32),
        "output_weight": scatter_about(key_of[7], (D, D), (max(D // 48, 4)) ** -0.5, 1.5, ((0, 2), (1, 2))),
        "output_bias": scatter_about(key_of[8], (D,), 0.5, 3.0, ((0, 2),), jnp.float32),
        "second_gain": jnp.clip(1.0 + 0.1 * jax.random.normal(key_of[9], (D,), jnp.float32), 0.5, 1.5),
        "second_shift": scatter_about(key_of[10], (D,), 0.5, 3.0, ((0, 2),), jnp.float32),
        "hidden_weight": draw_hidden_weight(jax.random.fold_in(key_of[15], 71), 0),
        "hidden_bias": scatter_about(key_of[12], (FF,), 0.5, 3.0, ((0, 2),), jnp.float32),
        "return_weight": scatter_about(key_of[13], (FF, D), (FF // 4) ** -0.5, 0.21875, ((0, 2), (1, 2))),
        "return_bias": scatter_about(key_of[14], (D,), 0.5, 3.0, ((0, 2),), jnp.float32),
    }


EPSILON = 1e-05

def rounded(values):
    return lax.optimization_barrier(values.astype(jnp.bfloat16))

def norm_forward(values, norm_gain, norm_shift):
    feature_count = values.shape[-1]
    mean_val = lax.optimization_barrier(jnp.sum(values, -1, keepdims=True)) / feature_count
    mean_square = lax.optimization_barrier(jnp.sum(values * values, -1, keepdims=True)) / feature_count
    inv_std = lax.rsqrt(mean_square - mean_val * mean_val + EPSILON)
    normed = (values - mean_val) * inv_std
    return (normed * norm_gain + norm_shift, normed, inv_std)

def norm_backward(upstream, normed, inv_std, norm_gain):
    feature_count = normed.shape[-1]
    scaled = upstream * norm_gain
    mean_first = lax.optimization_barrier(jnp.sum(scaled, -1, keepdims=True)) / feature_count
    mean_second = lax.optimization_barrier(jnp.sum(scaled * normed, -1, keepdims=True)) / feature_count
    return inv_std * (scaled - mean_first - normed * mean_second)

def gelu_tanh(values):
    return jax.nn.gelu(values, approximate=True)

def allowed_pairs(segments):
    length = segments.shape[-1]
    positions = jnp.arange(length)
    causal = positions[:, None] >= positions[None, :]
    same_doc = segments[:, :, None] == segments[:, None, :]
    return jnp.logical_and(causal[None], same_doc)[:, None]

def attention_logits(queries, keys_in):
    score_scale = 1.0 / math.sqrt(queries.shape[-1])
    return jnp.einsum('bqhd,bkhd->bhqk', queries.astype(jnp.float32), keys_in.astype(jnp.float32)) * score_scale

def attention_forward(queries, keys_in, values_in, segments):
    allowed = allowed_pairs(segments)
    logits = attention_logits(queries, keys_in)
    sum_total = lax.optimization_barrier(jnp.sum(jnp.where(allowed, jnp.exp(logits), 0.0), -1, keepdims=True))
    log_total = jnp.log(sum_total)
    probabilities = jnp.where(allowed, jnp.exp(logits - log_total), 0.0)
    prob_round = rounded(probabilities).astype(jnp.float32)
    attended = jnp.einsum('bhqk,bkhd->bqhd', prob_round, values_in.astype(jnp.float32))
    return (attended.astype(jnp.bfloat16), log_total)

def attention_backward(queries, keys_in, values_in, attended, attended_grad, log_total, segments):
    allowed = allowed_pairs(segments)
    logits = attention_logits(queries, keys_in)
    probabilities = jnp.where(allowed, jnp.exp(logits - log_total), 0.0)
    prob_round = rounded(probabilities).astype(jnp.float32)
    grad_full = attended_grad.astype(jnp.float32)
    value_grad = jnp.einsum('bhqk,bqhd->bkhd', prob_round, grad_full).astype(jnp.bfloat16)
    prob_grad = jnp.einsum('bqhd,bkhd->bhqk', grad_full, values_in.astype(jnp.float32))
    row_delta = jnp.transpose(lax.optimization_barrier(jnp.sum(grad_full * attended.astype(jnp.float32), -1)), (0, 2, 1))[..., None]
    logit_grad = rounded(probabilities * (prob_grad - row_delta)).astype(jnp.float32)
    score_scale = 1.0 / math.sqrt(queries.shape[-1])
    query_grad = (jnp.einsum('bhqk,bkhd->bqhd', logit_grad, keys_in.astype(jnp.float32)) * score_scale).astype(jnp.bfloat16)
    key_grad = (jnp.einsum('bhqk,bqhd->bkhd', logit_grad, queries.astype(jnp.float32)) * score_scale).astype(jnp.bfloat16)
    return (query_grad, key_grad, value_grad)

def run_block(params, block_in, block_cot, block_seg):
    first_gain, first_shift, input_weight, query_value_bias, output_weight, output_bias, second_gain, second_shift, hidden_weight, hidden_bias, return_weight, return_bias = params
    seq_count = block_seg.shape[0]
    length = block_seg.shape[1]
    residual = block_in.astype(jnp.float32)
    normed_in, first_hat, first_inv = norm_forward(residual, first_gain, first_shift)
    normed_round = normed_in.astype(jnp.bfloat16)
    flat_weight = input_weight.reshape(D, 3 * D)
    projected = jnp.dot(normed_round, flat_weight, preferred_element_type=jnp.float32).reshape(-1, 3, D)
    queries = (projected[:, 0] + query_value_bias[0]).astype(jnp.bfloat16)
    keys_all = projected[:, 1].astype(jnp.bfloat16)
    values_all = (projected[:, 2] + query_value_bias[1]).astype(jnp.bfloat16)
    query_four = queries.reshape(seq_count, length, HEADS, HEAD)
    key_four = keys_all.reshape(seq_count, length, HEADS, HEAD)
    value_four = values_all.reshape(seq_count, length, HEADS, HEAD)
    attended, log_total = attention_forward(query_four, key_four, value_four, block_seg)
    attended_flat = attended.reshape(-1, D)
    mixed = residual + jnp.dot(attended_flat, output_weight, preferred_element_type=jnp.float32) + output_bias
    normed_mid, second_hat, second_inv = norm_forward(mixed, second_gain, second_shift)
    middle_round = normed_mid.astype(jnp.bfloat16)
    hidden_pre = jnp.dot(middle_round, hidden_weight, preferred_element_type=jnp.float32) + hidden_bias
    hidden_act, gelu_back = jax.vjp(gelu_tanh, hidden_pre)
    hidden_round = hidden_act.astype(jnp.bfloat16)
    output = (mixed + jnp.dot(hidden_round, return_weight, preferred_element_type=jnp.float32) + return_bias).astype(jnp.bfloat16)
    upstream = block_cot.astype(jnp.float32)
    return_weight_grad = jnp.dot(hidden_round.T, block_cot, preferred_element_type=jnp.float32)
    return_bias_grad = lax.optimization_barrier(jnp.sum(upstream, 0))
    act_grad = jnp.dot(block_cot, return_weight.T, preferred_element_type=jnp.float32)
    pre_grad = gelu_back(act_grad)[0].astype(jnp.bfloat16)
    hidden_weight_grad = jnp.dot(middle_round.T, pre_grad, preferred_element_type=jnp.float32)
    hidden_bias_grad = lax.optimization_barrier(jnp.sum(pre_grad.astype(jnp.float32), 0))
    middle_grad = jnp.dot(pre_grad, hidden_weight.T, preferred_element_type=jnp.float32)
    second_gain_grad = lax.optimization_barrier(jnp.sum(middle_grad * second_hat, 0))
    second_shift_grad = lax.optimization_barrier(jnp.sum(middle_grad, 0))
    mixed_grad = upstream + norm_backward(middle_grad, second_hat, second_inv, second_gain)
    mixed_round = mixed_grad.astype(jnp.bfloat16)
    output_weight_grad = jnp.dot(attended_flat.T, mixed_round, preferred_element_type=jnp.float32)
    output_bias_grad = lax.optimization_barrier(jnp.sum(mixed_grad, 0))
    attended_grad = jnp.dot(mixed_round, output_weight.T, preferred_element_type=jnp.float32).astype(jnp.bfloat16)
    query_grad, key_grad, value_grad = attention_backward(query_four, key_four, value_four, attended, attended_grad.reshape(seq_count, length, HEADS, HEAD), log_total, block_seg)
    query_flat = query_grad.reshape(-1, D)
    value_flat = value_grad.reshape(-1, D)
    stacked = jnp.stack([query_flat, key_grad.reshape(-1, D), value_flat], axis=1)
    stacked_flat = stacked.reshape(-1, 3 * D)
    input_weight_grad = jnp.dot(normed_round.T, stacked_flat, preferred_element_type=jnp.float32).reshape(D, 3, D)
    bias_grad = jnp.stack([lax.optimization_barrier(jnp.sum(query_flat.astype(jnp.float32), 0)), lax.optimization_barrier(jnp.sum(value_flat.astype(jnp.float32), 0))])
    normed_grad = jnp.dot(stacked_flat, flat_weight.T, preferred_element_type=jnp.float32)
    first_gain_grad = lax.optimization_barrier(jnp.sum(normed_grad * first_hat, 0))
    first_shift_grad = lax.optimization_barrier(jnp.sum(normed_grad, 0))
    input_grad = (mixed_grad + norm_backward(normed_grad, first_hat, first_inv, first_gain)).astype(jnp.bfloat16)
    grads = (first_gain_grad, first_shift_grad, input_weight_grad, bias_grad, output_weight_grad, output_bias_grad, second_gain_grad, second_shift_grad, hidden_weight_grad, hidden_bias_grad, return_weight_grad, return_bias_grad)
    return (output, input_grad, grads)

def reference(block_input, cotangent, segment_ids, first_gain, first_shift, input_weight, query_value_bias, output_weight, output_bias, second_gain, second_shift, hidden_weight, hidden_bias, return_weight, return_bias):
    params = (first_gain, first_shift, input_weight, query_value_bias, output_weight, output_bias, second_gain, second_shift, hidden_weight, hidden_bias, return_weight, return_bias)
    block_seqs = math.gcd(SEQS, 8)
    blocks = SEQS // block_seqs
    block_rows = block_seqs * SEQ
    inputs_split = block_input.reshape(blocks, block_rows, D)
    cot_split = cotangent.reshape(blocks, block_rows, D)
    seg_split = segment_ids.reshape(blocks, block_seqs, SEQ)

    def scan_step(running, sliced):
        output, input_grad, grads = run_block(params, sliced[0], sliced[1], sliced[2])
        return (jax.tree.map(jnp.add, running, grads), (output, input_grad))
    initial = tuple((jnp.zeros(param.shape, jnp.float32) for param in params))
    running, (outputs, input_grads) = lax.scan(scan_step, initial, (inputs_split, cot_split, seg_split))
    first_gain_grad, first_shift_grad, input_weight_grad, bias_grad, output_weight_grad, output_bias_grad, second_gain_grad, second_shift_grad, hidden_weight_grad, hidden_bias_grad, return_weight_grad, return_bias_grad = running
    return (outputs.reshape(TOKENS, D), input_grads.reshape(TOKENS, D), first_gain_grad, first_shift_grad, input_weight_grad, bias_grad, output_weight_grad, output_bias_grad, second_gain_grad, second_shift_grad, hidden_weight_grad, hidden_bias_grad, return_weight_grad, return_bias_grad)
```

```python
import math

import jax
import jax.numpy as jnp
from jax import lax
from jax.experimental import pallas as pl
from jax.experimental.pallas import tpu as pltpu
from jax.sharding import PartitionSpec as P

HEAD = 64
PAIR = 128
EPSILON = 1e-05
BF = jnp.bfloat16
F32 = jnp.float32

GATHER_A = ((0, 2), (1, 0), (2, 3), (3, 1))
GATHER_B = ((1, 2), (2, 1))
RETURN_ROW = ((2, 0), (1, 3))
SWAP = ((0, 1), (1, 0))


def nn(a, b):
    return lax.dot_general(a, b, (((1,), (0,)), ((), ())), preferred_element_type=F32)


def nt(a, b):
    return lax.dot_general(a, b, (((1,), (1,)), ((), ())), preferred_element_type=F32)


def tn(a, b):
    return lax.dot_general(a, b, (((0,), (0,)), ((), ())), preferred_element_type=F32)


def vmem():
    return pl.BlockSpec(memory_space=pltpu.VMEM)


def smem():
    return pl.BlockSpec(memory_space=pltpu.SMEM)


def call(body, name, ins, outs, scalars=1, scratch=()):
    specs = [smem()] * scalars + [vmem()] * (len(ins) - scalars)
    return pl.pallas_call(
        body,
        name=name,
        out_shape=[jax.ShapeDtypeStruct(s, d) for s, d in outs],
        in_specs=specs,
        out_specs=[vmem()] * len(outs),
        scratch_shapes=list(scratch),
    )(*ins)


def stats(own, oth):
    width = own.shape[1] + oth.shape[1]
    mean = (jnp.sum(own, -1, keepdims=True) + jnp.sum(oth, -1, keepdims=True)) / width
    square = (
        jnp.sum(own * own, -1, keepdims=True) + jnp.sum(oth * oth, -1, keepdims=True)
    ) / width
    inv = lax.rsqrt(square - mean * mean + EPSILON)
    return mean, inv


def norm_back(grad_own, grad_oth, hat_own, hat_oth, inv, gain_own, gain_oth):
    width = grad_own.shape[1] + grad_oth.shape[1]
    s_own = grad_own * gain_own
    s_oth = grad_oth * gain_oth
    first = (jnp.sum(s_own, -1, keepdims=True) + jnp.sum(s_oth, -1, keepdims=True)) / width
    second = (
        jnp.sum(s_own * hat_own, -1, keepdims=True) + jnp.sum(s_oth * hat_oth, -1, keepdims=True)
    ) / width
    return (
        inv * (s_own - first - hat_own * second),
        inv * (s_oth - first - hat_oth * second),
    )


def allowed_mask(seg_col, seg_row):
    shape = (seg_col.shape[0], seg_row.shape[1])
    rows = lax.broadcasted_iota(jnp.int32, shape, 0)
    cols = lax.broadcasted_iota(jnp.int32, shape, 1)
    return jnp.logical_and(rows >= cols, seg_col == seg_row)


G1, S1, OB, G2, S2, RB = range(6)


def forward_kernel(
    flag, x_ref, a_ref, b_ref, win_own, win_oth, vec, qvb, seg_col, seg_row, wout_own, wout_oth,
    xs_ref, h1_ref, qkv_ref, att_ref, lt_ref, part_ref,
):
    same = flag[0] == 1
    x_in, a_in, b_in = x_ref[...], a_ref[...], b_ref[...]
    x_own = jnp.where(same, x_in, a_in)
    x_oth = jnp.where(same, a_in, b_in)
    xs_ref[0] = x_own
    xs_ref[1] = x_oth
    x_own = x_own.astype(F32)
    x_oth = x_oth.astype(F32)
    mean, inv = stats(x_own, x_oth)
    h_own = ((x_own - mean) * inv * vec[0, G1:G1 + 1] + vec[0, S1:S1 + 1]).astype(BF)
    h_oth = ((x_oth - mean) * inv * vec[1, G1:G1 + 1] + vec[1, S1:S1 + 1]).astype(BF)
    h1_ref[0] = h_own
    h1_ref[1] = h_oth
    width = h_own.shape[1]
    for j in range(3):
        cut = slice(j * width, (j + 1) * width)
        proj = nn(h_own, win_own[:, cut]) + nn(h_oth, win_oth[:, cut])
        if j == 0:
            proj = proj + qvb[0:1]
        if j == 2:
            proj = proj + qvb[1:2]
        qkv_ref[:, cut] = proj.astype(BF)
    allowed = allowed_mask(seg_col[...], seg_row[...])
    lanes = lax.broadcasted_iota(jnp.int32, (x_own.shape[0], PAIR), 1)
    totals = jnp.zeros((x_own.shape[0], PAIR), F32)
    scale = 1.0 / math.sqrt(HEAD)
    for p in range(width // PAIR):
        q2 = qkv_ref[:, p * PAIR:(p + 1) * PAIR]
        k2 = qkv_ref[:, width + p * PAIR:width + (p + 1) * PAIR]
        v2 = qkv_ref[:, 2 * width + p * PAIR:2 * width + (p + 1) * PAIR]
        done = []
        for e in range(2):
            inside = (lanes // HEAD) == e
            logits = nt(jnp.where(inside, q2, jnp.zeros_like(q2)), k2) * scale
            total = jnp.sum(jnp.where(allowed, jnp.exp(logits), 0.0), -1, keepdims=True)
            log_total = jnp.log(total)
            probs = jnp.where(allowed, jnp.exp(logits - log_total), 0.0).astype(BF)
            done.append(nn(probs, v2))
            totals = jnp.where(lanes == 2 * p + e, log_total, totals)
        att_ref[:, p * PAIR:(p + 1) * PAIR] = jnp.where(lanes < HEAD, done[0], done[1]).astype(BF)
    lt_ref[...] = totals
    attended = att_ref[...]
    part_ref[0] = nn(attended, wout_own[...]).astype(BF)
    part_ref[1] = nn(attended, wout_oth[...]).astype(BF)


def act_grad_kernel(flag, x_ref, a_ref, b_ref, wret_own, wret_oth, cots_ref, grad_ref):
    same = flag[0] == 1
    x_in, a_in, b_in = x_ref[...], a_ref[...], b_ref[...]
    own = jnp.where(same, x_in, a_in)
    oth = jnp.where(same, a_in, b_in)
    cots_ref[0] = own
    cots_ref[1] = oth
    grad_ref[...] = nt(own, wret_own[...]) + nt(oth, wret_oth[...])


def mixed_of(xs, part, recv, vec):
    own = xs[0].astype(F32) + (part[0].astype(F32) + recv[0].astype(F32)) + vec[0, OB:OB + 1]
    oth = xs[1].astype(F32) + (part[1].astype(F32) + recv[1].astype(F32)) + vec[1, OB:OB + 1]
    return own, oth


def middle_kernel(
    xs, part, recv, vec, whid_own, whid_oth, hbias, act_grad,
    h2_ref, act_ref, pre_ref, down_ref,
):
    m_own, m_oth = mixed_of(xs, part, recv, vec)
    mean, inv = stats(m_own, m_oth)
    h_own = ((m_own - mean) * inv * vec[0, G2:G2 + 1] + vec[0, S2:S2 + 1]).astype(BF)
    h_oth = ((m_oth - mean) * inv * vec[1, G2:G2 + 1] + vec[1, S2:S2 + 1]).astype(BF)
    h2_ref[0] = h_own
    h2_ref[1] = h_oth
    hidden = hbias.shape[1]
    step = 512 if hidden % 512 == 0 else hidden
    root = math.sqrt(2.0 / math.pi)
    for j in range(hidden // step):
        cut = slice(j * step, (j + 1) * step)
        u = nn(h_own, whid_own[:, cut]) + nn(h_oth, whid_oth[:, cut]) + hbias[:, cut]
        square = u * u
        t = jnp.tanh(root * (u + 0.044715 * (u * square)))
        act_ref[:, cut] = (0.5 * u * (1.0 + t)).astype(BF)
        slope = 0.5 * (1.0 + t) + 0.5 * u * (1.0 - t * t) * (root * (1.0 + 0.134145 * square))
        pre_ref[:, cut] = (act_grad[:, cut] * slope).astype(BF)
    pre = pre_ref[...]
    down_ref[0] = nt(pre, whid_own[...]).astype(BF)
    down_ref[1] = nt(pre, whid_oth[...]).astype(BF)


def out_kernel(act, pre, wret_own, wret_oth, out_ref, bias_ref):
    rounded = act[...]
    out_ref[0] = nn(rounded, wret_own[...]).astype(BF)
    out_ref[1] = nn(rounded, wret_oth[...]).astype(BF)
    bias_ref[...] = jnp.sum(pre[...].astype(F32), 0, keepdims=True)


def backward_kernel(
    xs, part, recv, vec, down, down_recv, cots, qkv, att, lt, seg_col, seg_row, wout_own, wout_oth,
    mg_ref, mr_ref, dproj_ref, wide_ref, heads_ref,
):
    m_own, m_oth = mixed_of(xs, part, recv, vec)
    mean, inv = stats(m_own, m_oth)
    hat_own = (m_own - mean) * inv
    hat_oth = (m_oth - mean) * inv
    g_own = down[0].astype(F32) + down_recv[0].astype(F32)
    g_oth = down[1].astype(F32) + down_recv[1].astype(F32)
    c_own = cots[0].astype(F32)
    c_oth = cots[1].astype(F32)
    b_own, b_oth = norm_back(g_own, g_oth, hat_own, hat_oth, inv, vec[0, G2:G2 + 1], vec[1, G2:G2 + 1])
    b_own = c_own + b_own
    b_oth = c_oth + b_oth
    mg_ref[0] = b_own
    mg_ref[1] = b_oth
    r_own = b_own.astype(BF)
    r_oth = b_oth.astype(BF)
    mr_ref[0] = r_own
    mr_ref[1] = r_oth
    for i, (g, hat, b, c) in enumerate(
        ((g_own, hat_own, b_own, c_own), (g_oth, hat_oth, b_oth, c_oth))
    ):
        wide_ref[i, 0:1] = jnp.sum(g * hat, 0, keepdims=True)
        wide_ref[i, 1:2] = jnp.sum(g, 0, keepdims=True)
        wide_ref[i, 2:3] = jnp.sum(b, 0, keepdims=True)
        wide_ref[i, 3:4] = jnp.sum(c, 0, keepdims=True)
    ag = (nt(r_own, wout_own[...]) + nt(r_oth, wout_oth[...])).astype(BF)
    width = ag.shape[1]
    allowed = allowed_mask(seg_col[...], seg_row[...])
    lanes = lax.broadcasted_iota(jnp.int32, (ag.shape[0], PAIR), 1)
    scale = 1.0 / math.sqrt(HEAD)
    for p in range(width // PAIR):
        cut = slice(p * PAIR, (p + 1) * PAIR)
        q2 = qkv[:, cut]
        k2 = qkv[:, width + p * PAIR:width + (p + 1) * PAIR]
        v2 = qkv[:, 2 * width + p * PAIR:2 * width + (p + 1) * PAIR]
        ag2 = ag[:, cut]
        product = ag2.astype(F32) * att[:, cut].astype(F32)
        dq, dk, dv = [], [], []
        for e in range(2):
            inside = (lanes // HEAD) == e
            zero = jnp.zeros_like(q2)
            logits = nt(jnp.where(inside, q2, zero), k2) * scale
            log_total = lt[:, 2 * p + e:2 * p + e + 1]
            probs = jnp.where(allowed, jnp.exp(logits - log_total), 0.0)
            dv.append(tn(probs.astype(BF), ag2))
            prob_grad = nt(jnp.where(inside, ag2, zero), v2)
            delta = jnp.sum(jnp.where(inside, product, 0.0), -1, keepdims=True)
            logit_grad = (probs * (prob_grad - delta)).astype(BF)
            dq.append(nn(logit_grad, k2))
            dk.append(tn(logit_grad, q2))
        left = lanes < HEAD
        dq = (jnp.where(left, dq[0], dq[1]) * scale).astype(BF)
        dk = (jnp.where(left, dk[0], dk[1]) * scale).astype(BF)
        dv = jnp.where(left, dv[0], dv[1]).astype(BF)
        dproj_ref[:, cut] = dq
        dproj_ref[:, width + p * PAIR:width + (p + 1) * PAIR] = dk
        dproj_ref[:, 2 * width + p * PAIR:2 * width + (p + 1) * PAIR] = dv
        heads_ref[0:1, cut] = jnp.sum(dq.astype(F32), 0, keepdims=True)
        heads_ref[1:2, cut] = jnp.sum(dv.astype(F32), 0, keepdims=True)


def input_kernel(xs, dproj, win_own, win_oth, part_ref, wide_ref):
    x_own = xs[0].astype(F32)
    x_oth = xs[1].astype(F32)
    mean, inv = stats(x_own, x_oth)
    grads = dproj[...]
    for i, (x, w) in enumerate(((x_own, win_own), (x_oth, win_oth))):
        g = nt(grads, w[...])
        part_ref[i] = g.astype(BF)
        wide_ref[i, 0:1] = jnp.sum(g * ((x - mean) * inv), 0, keepdims=True)
        wide_ref[i, 1:2] = jnp.sum(g, 0, keepdims=True)


def last_kernel(
    xs, part, recv, vec, out_part, out_recv, mg, h1g, h1g_recv, both_ref,
):
    m = mixed_of(xs, part, recv, vec)
    for i in range(2):
        both_ref[0, i] = (
            m[i] + (out_part[i].astype(F32) + out_recv[i].astype(F32)) + vec[i, RB:RB + 1]
        ).astype(BF)
    x_own = xs[0].astype(F32)
    x_oth = xs[1].astype(F32)
    mean, inv = stats(x_own, x_oth)
    g_own = h1g[0].astype(F32) + h1g_recv[0].astype(F32)
    g_oth = h1g[1].astype(F32) + h1g_recv[1].astype(F32)
    b_own, b_oth = norm_back(
        g_own, g_oth, (x_own - mean) * inv, (x_oth - mean) * inv, inv,
        vec[0, G1:G1 + 1], vec[1, G1:G1 + 1],
    )
    both_ref[1, 0] = (mg[0] + b_own).astype(BF)
    both_ref[1, 1] = (mg[1] + b_oth).astype(BF)


def grad_kernel(bit, lhs, rhs, lhs_recv, rhs_recv, send_ref, keep_ref, full):
    half = keep_ref.shape[0]
    full[...] = tn(lhs[...], rhs[...]) + tn(lhs_recv[...], rhs_recv[...])
    keep_at = pl.multiple_of(bit[0] * half, 8)
    send_at = pl.multiple_of((1 - bit[0]) * half, 8)
    send_ref[...] = full[pl.ds(send_at, half), :].astype(BF)
    keep_ref[...] = full[pl.ds(keep_at, half), :]


def weight_grad(name, bit, lhs, rhs, lhs_recv, rhs_recv):
    rows, cols = lhs.shape[1], rhs.shape[1]
    return call(
        grad_kernel, name, (bit, lhs, rhs, lhs_recv, rhs_recv),
        [((rows // 2, cols), BF), ((rows // 2, cols), F32)],
        scratch=[pltpu.VMEM((rows, cols), F32)],
    )


def shards(
    block_input, cotangent, segment_ids, first_gain, first_shift, input_weight, query_value_bias,
    output_weight, output_bias, second_gain, second_shift, hidden_weight, hidden_bias,
    return_weight, return_bias, *, groups,
):
    row = lax.axis_index("row")
    col = lax.axis_index("col")
    me = lax.axis_index("dp")
    bits = groups.bit_length() - 1
    tokens, half = block_input.shape
    heads_width = input_weight.shape[2]
    hidden = hidden_bias.shape[0]
    same = row == col
    flag = same.astype(jnp.int32).reshape(1)

    def swap_col(value):
        return lax.ppermute(value, "col", SWAP)

    def swap_row(value):
        return lax.ppermute(value, "row", SWAP)

    def group(value, pairs):
        return lax.ppermute(value, ("row", "col"), pairs)

    def over_dp(value, b):
        return lax.ppermute(value, "dp", [(i, i ^ (1 << b)) for i in range(groups)])

    def bit_of(b):
        return (me >> b) & 1

    x_a = group(block_input, GATHER_A)
    x_b = group(block_input, GATHER_B)
    win_own = input_weight.reshape(half, 3 * heads_width)
    win_oth = swap_col(win_own)
    vec_own = jnp.stack([first_gain, first_shift, output_bias, second_gain, second_shift, return_bias])
    vec = jnp.stack([vec_own, swap_col(vec_own)])
    wout_oth = swap_col(output_weight)
    wret_oth = swap_col(return_weight)
    whid_oth = swap_col(hidden_weight)
    c_a = group(cotangent, GATHER_A)
    c_b = group(cotangent, GATHER_B)
    seg_col = segment_ids.reshape(tokens, 1)
    seg_row = segment_ids.reshape(1, tokens)

    wide = ((2, tokens, half), BF)
    xs, h1, qkv, att, lt, part = call(
        forward_kernel, "fwd_attention",
        (flag, block_input, x_a, x_b, win_own, win_oth, vec, query_value_bias, seg_col, seg_row,
         output_weight, wout_oth),
        [wide, wide, ((tokens, 3 * heads_width), BF), ((tokens, heads_width), BF),
         ((tokens, PAIR), F32), wide],
    )
    recv = swap_row(part)
    cots, act_grad = call(
        act_grad_kernel, "act_grad", (flag, cotangent, c_a, c_b, return_weight, wret_oth),
        [wide, ((tokens, hidden), F32)],
    )
    h2, act, pre, down = call(
        middle_kernel, "middle",
        (xs, part, recv, vec, hidden_weight, whid_oth, hidden_bias.reshape(1, hidden), act_grad),
        [wide, ((tokens, hidden), BF), ((tokens, hidden), BF), wide], scalars=0,
    )
    down_recv = swap_row(down)
    act_recv = swap_col(act)
    cot_recv = swap_col(cots[1])
    pre_recv = swap_col(pre)
    h2_recv = swap_col(h2[1])
    out_part, hbias_sum = call(
        out_kernel, "out_part", (act, pre, return_weight, wret_oth), [wide, ((1, hidden), F32)],
        scalars=0,
    )

    def reduce_start(name, order, lhs, rhs, lhs_recv, rhs_recv):
        bit = bit_of(order[0]).astype(jnp.int32).reshape(1)
        send, keep = weight_grad(name, bit, lhs, rhs, lhs_recv, rhs_recv)
        total = keep + over_dp(send, order[0]).astype(F32)
        for b in order[1:]:
            size = total.shape[0] // 2
            bit = bit_of(b)
            keep = lax.dynamic_slice_in_dim(total, bit * size, size, 0)
            send = lax.dynamic_slice_in_dim(total, (1 - bit) * size, size, 0).astype(BF)
            total = keep + over_dp(send, b).astype(F32)
        return total.astype(BF)

    def gather_end(value, order):
        for b in reversed(order):
            other = over_dp(value, b)
            low = bit_of(b) == 0
            value = jnp.concatenate([jnp.where(low, value, other), jnp.where(low, other, value)], 0)
        return value.astype(F32)

    order_a = tuple(range(bits))
    order_c = (1, 0) + order_a[2:] if bits > 1 else order_a
    ret = gather_end(reduce_start("ret_grad", order_a, act, cots[0], act_recv, cot_recv), order_a)
    hid = gather_end(reduce_start("hid_grad", order_c, h2[0], pre, h2_recv, pre_recv), order_c)

    mg, mr, dproj, wide_mid, heads_sum = call(
        backward_kernel, "bwd_attention",
        (xs, part, recv, vec, down, down_recv, cots, qkv, att, lt, seg_col, seg_row, output_weight,
         wout_oth),
        [((2, tokens, half), F32), wide, ((tokens, 3 * heads_width), BF), ((2, 4, half), F32),
         ((2, heads_width), F32)],
        scalars=0,
    )
    dproj_recv = swap_col(dproj)
    h1_recv = swap_col(h1[1])
    att_recv = swap_col(att)
    mr_recv = swap_col(mr[1])
    h1g, wide_first = call(
        input_kernel, "input_part", (xs, dproj, win_own, win_oth), [wide, ((2, 2, half), F32)],
        scalars=0,
    )
    out_recv = group(out_part, RETURN_ROW)
    h1g_recv = group(h1g, RETURN_ROW)
    (both,) = call(
        last_kernel, "last", (xs, part, recv, vec, out_part, out_recv, mg, h1g, h1g_recv),
        [((2, 2, tokens, half), BF)], scalars=0,
    )
    finish = jnp.where(same, both[:, 0], swap_col(both[:, 1]))

    win = gather_end(reduce_start("in_grad", order_a, h1[0], dproj, h1_recv, dproj_recv), order_a)
    wout = gather_end(reduce_start("out_grad", order_c, att, mr[0], att_recv, mr_recv), order_c)

    widths = jnp.concatenate([wide_first, 0.5 * wide_mid], 1)
    widths = widths[0] + swap_col(widths[1])
    widths = widths + swap_row(widths)
    rows = jnp.concatenate([hbias_sum.reshape(-1), heads_sum.reshape(-1)])
    rows = rows + swap_col(rows)
    small = jnp.concatenate([widths.reshape(-1), rows]).reshape(-1, PAIR)
    for b in range(bits):
        small = small + over_dp(small, b)
    small = small.reshape(-1)
    widths = small[:6 * half].reshape(6, half)
    hidden_bias_grad = small[6 * half:6 * half + hidden]
    bias_grad = small[6 * half + hidden:].reshape(2, heads_width)
    return (
        finish[0],
        finish[1],
        widths[0],
        widths[1],
        win.reshape(half, 3, heads_width),
        bias_grad,
        wout,
        widths[4],
        widths[2],
        widths[3],
        hid,
        hidden_bias_grad,
        ret,
        widths[5],
    )


def solution(mesh):
    groups = mesh.shape["dp"]

    def body(*args):
        return shards(*args, groups=groups)

    return jax.shard_map(
        body,
        mesh=mesh,
        in_specs=(
            P(("dp", "row"), "col"),
            P(("dp", "row"), "col"),
            P(("dp", "col"), None),
            P("col"),
            P("col"),
            P("col", None, "row"),
            P(None, "row"),
            P("row", "col"),
            P("col"),
            P("col"),
            P("col"),
            P("col", "row"),
            P("row"),
            P("row", "col"),
            P("col"),
        ),
        out_specs=(
            P(("dp", "row"), "col"),
            P(("dp", "row"), "col"),
            P("col"),
            P("col"),
            P("col", None, "row"),
            P(None, "row"),
            P("row", "col"),
            P("col"),
            P("col"),
            P("col"),
            P("col", "row"),
            P("row"),
            P("row", "col"),
            P("col"),
        ),
        check_vma=False,
    )
```
